32 devices in a mesh: head: 4 (over z), tok: 8 (over y, x, core).
Axes of the slice: x: 2, y: 2, z: 4, core: 2. Of those that a mesh axis runs over, the one named last changes fastest.
Arguments:
- teacher_q: bfloat16 [1024, 1024], P('tok', 'head'), may hold values from -48 to 48
- student_q: bfloat16 [1024, 1024], P('tok', 'head'), may hold values from -48 to 48
- owner_table: int32 [8, 8], replicated, may hold values from -1 to 7, as said below
Outputs:
- student_grad: bfloat16 [1024, 1024], P('tok', 'head')
- divergence: float32 [16], P('head')
The draws below stay inside these ranges and needn't reach their ends.
Inputs may be any that keep to these rules, and one draw needn't show every extreme that they name: `owner_table`: Symmetric; every diagonal entry is an owner; an owner is a tok index; each tok index owns at most 2 pairs i <= j, and some tok index owns exactly 2 in every draw.
All inputs are finite; a program needn't handle non-finite values.
Results may differ from the reference program's by a relative error of at most 0.0049.
Values may be sent and summed in bfloat16 or wider, within the bound.
A program may use at most 64 MiB of HBM per device.

```python
import jax
import jax.numpy as jnp
import numpy as np
from jax import lax

HEAD_DIM = 64
TOK_DEV = 128
REL_HEADS = 16
TOKENS = 1024
BLOCKS = 8
PAIR_MOST = 2


def draw_queries(key):
    base = jnp.clip(jax.random.normal(key, (TOKENS, REL_HEADS, HEAD_DIM)), -6.0, 6.0)
    return base.reshape(TOKENS, REL_HEADS * HEAD_DIM).astype(jnp.bfloat16)


def draw_teacher_q(key, part):
    return draw_queries(jax.random.fold_in(key, 11))


def draw_student_q(key, part):
    return draw_queries(jax.random.fold_in(key, 23))


def draw_owner_table(key, part):
    upper_rows, upper_cols = np.triu_indices(BLOCKS)
    every_place = np.arange(upper_rows.shape[0])
    diagonal_places = every_place[upper_rows == upper_cols]
    other_places = every_place[upper_rows != upper_cols]
    key_diag, key_other, key_caps, key_owner = jax.random.split(jax.random.fold_in(key, 7), 4)
    ordering = jnp.concatenate([jax.random.permutation(key_diag, jnp.asarray(diagonal_places, jnp.int32)), jax.random.permutation(key_other, jnp.asarray(other_places, jnp.int32))])
    capacity = jax.random.randint(key_caps, (BLOCKS,), 1, PAIR_MOST + 1).astype(jnp.int32).at[0].set(PAIR_MOST)
    owners_order = jax.random.permutation(key_owner, BLOCKS).astype(jnp.int32)
    bounds = jnp.cumsum(capacity)
    positions = jnp.arange(upper_rows.shape[0], dtype=jnp.int32)
    which = jnp.sum((bounds[None, :] <= positions[:, None]).astype(jnp.int32), axis=1)
    owners = jnp.where(which < BLOCKS, owners_order[jnp.minimum(which, BLOCKS - 1)], -1)
    pair_rows = jnp.asarray(upper_rows, jnp.int32)[ordering]
    pair_cols = jnp.asarray(upper_cols, jnp.int32)[ordering]
    table = jnp.full((BLOCKS, BLOCKS), -1, jnp.int32)
    table = table.at[pair_rows, pair_cols].set(owners)
    return table.at[pair_cols, pair_rows].set(owners)


def setup_inputs(seed: int = 0) -> dict:
    splits = jax.random.split(jax.random.key(seed), 4)
    teacher_q = draw_teacher_q(jax.random.fold_in(splits[3], 71), 0)
    student_q = draw_student_q(jax.random.fold_in(splits[3], 71), 0)
    owner_table = draw_owner_table(jax.random.fold_in(splits[3], 71), 0)
    return {"teacher_q": teacher_q, "student_q": student_q, "owner_table": owner_table}


floor_value = -1e+30
distill_weight = 32.0

def reference(teacher_q, student_q, owner_table):
    scale = HEAD_DIM ** (-0.5)
    length = teacher_q.shape[0]
    inside = jnp.repeat(jnp.repeat(owner_table >= 0, TOK_DEV, axis=0), TOK_DEV, axis=1)
    heads_teacher = teacher_q.reshape(length, REL_HEADS, HEAD_DIM).transpose(1, 0, 2)
    heads_student = student_q.reshape(length, REL_HEADS, HEAD_DIM).transpose(1, 0, 2)

    def logsum(scores):
        masked = jnp.where(inside, scores, floor_value)
        highest = jnp.max(masked, axis=1)
        return highest + jnp.log(jnp.sum(jnp.exp(masked - highest[:, None]), axis=1))

    def one_head(queries):
        teacher_head, student_head = queries
        teacher_scores = jnp.dot(teacher_head.astype(jnp.float32), teacher_head.T.astype(jnp.float32), preferred_element_type=jnp.float32) * scale
        student_scores = jnp.dot(student_head.astype(jnp.float32), student_head.T.astype(jnp.float32), preferred_element_type=jnp.float32) * scale
        teacher_logsum = logsum(teacher_scores)
        student_logsum = logsum(student_scores)
        teacher_prob = jnp.where(inside, jnp.exp(teacher_scores - teacher_logsum[:, None]), 0.0)
        student_prob = jnp.where(inside, jnp.exp(student_scores - student_logsum[:, None]), 0.0)
        row_div = jnp.sum(teacher_prob * (teacher_scores - student_scores), axis=1) - teacher_logsum + student_logsum
        score_gap = student_prob - teacher_prob
        symmetric = (score_gap + score_gap.T).astype(jnp.bfloat16)
        gradient = jnp.dot(symmetric.astype(jnp.float32), student_head.astype(jnp.float32), preferred_element_type=jnp.float32) * (scale * distill_weight)
        return (gradient.astype(jnp.bfloat16), jnp.mean(row_div))
    gradients, divergence = lax.map(one_head, (heads_teacher, heads_student))
    return (gradients.transpose(1, 0, 2).reshape(length, REL_HEADS * HEAD_DIM), divergence)
```

```python
import functools
import math

import jax
import jax.numpy as jnp
from jax import lax
from jax.experimental import pallas as pl
from jax.experimental.pallas import tpu as pltpu
from jax.sharding import PartitionSpec as P

HEAD_DIM = 64
LANES = 128
floor_value = -1e30
distill_weight = 32.0
score_factor = HEAD_DIM ** (-0.5) * math.log2(math.e)
MESH = pl.DeviceIdType.MESH


def repeat(count, body, init=None):
    if count <= 8:
        for step in range(count):
            init = body(step, init)
        return init
    return lax.fori_loop(0, count, body, init)


def kernel(
    n, teacher_hbm, student_hbm, table, grad_ref, div_ref,
    teacher, student, own_teacher, own_student, t_scores, s_scores, t_top, s_top,
    t_log, s_log, row_part, stats, total,
    local_sem, send_sem, recv_sem, pass_send, pass_recv, stat_send, stat_recv,
):
    rows, width = teacher_hbm.shape
    pairs = width // LANES
    heads = width // HEAD_DIM
    group = LANES // HEAD_DIM
    chips = n // 2
    side = math.isqrt(chips)
    side = side if side * side == chips else 1
    span = chips // side
    me = lax.axis_index("tok")
    head_at = lax.axis_index("head")
    chip, core = me // 2, me % 2
    sibling = chip * 2 + 1 - core

    def spot(tok):
        return (head_at, tok)

    def shifted(k, sign):
        high = (chip // span + sign * (k // span) + side) % side
        low = (chip % span + sign * (k % span) + span) % span
        return high * span + low

    barrier = pltpu.get_barrier_semaphore()

    def greet(d, carry):
        pl.semaphore_signal(barrier, inc=1, device_id=spot((me + d + 1) % n), device_id_type=MESH)
        return carry

    loads = [
        pltpu.make_async_copy(teacher_hbm, teacher.at[me], local_sem.at[0]),
        pltpu.make_async_copy(student_hbm, student.at[me], local_sem.at[1]),
    ]
    for load in loads:
        load.start()
    repeat(n - 1, greet)
    sources = ((teacher_hbm, teacher), (student_hbm, student))

    def own_copy(which, k, target):
        return pltpu.make_async_remote_copy(
            src_ref=sources[which][0],
            dst_ref=sources[which][1].at[me],
            send_sem=send_sem.at[which, k],
            recv_sem=recv_sem.at[which, k],
            device_id=spot(target),
            device_id_type=MESH,
        )

    def pass_copy(which, k, source):
        buffer = sources[which][1]
        return pltpu.make_async_remote_copy(
            src_ref=buffer.at[source],
            dst_ref=buffer.at[source],
            send_sem=pass_send.at[which, k],
            recv_sem=pass_recv.at[which, k],
            device_id=spot(sibling),
            device_id_type=MESH,
        )

    pl.semaphore_wait(barrier, n - 1)

    def send_own(k, carry):
        for which in range(2):
            own_copy(which, k + 1, shifted(k + 1, 1) * 2 + core).start()
        return carry

    repeat(chips - 1, send_own)
    for which in range(2):
        own_copy(which, 0, sibling).start()

    for load in loads:
        load.wait()
    lane = lax.broadcasted_iota(jnp.int32, (rows, LANES), 1)
    for pair in range(pairs):
        for inner in range(group):
            at = pl.ds((pair * group + inner) * rows, rows)
            keep = lane // HEAD_DIM == inner
            columns = pl.ds(pair * LANES, LANES)
            own_teacher[at, :] = jnp.where(keep, teacher[me, :, columns], jnp.zeros((), jnp.bfloat16))
            own_student[at, :] = jnp.where(keep, student[me, :, columns], jnp.zeros((), jnp.bfloat16))

    def score(block, first):
        bias = jnp.where(table[me, block] >= 0, 0.0, floor_value).astype(jnp.float32)
        for own, whole, scores, top in (
            (own_teacher, teacher, t_scores, t_top),
            (own_student, student, s_scores, s_top),
        ):
            for pair in range(pairs):
                at = pl.ds(pair * group * rows, group * rows)
                raw = lax.dot_general(
                    own[at, :],
                    whole[block, :, pl.ds(pair * LANES, LANES)],
                    (((1,), (1,)), ((), ())),
                    preferred_element_type=jnp.float32,
                )
                tile = raw * score_factor + bias
                scores[block, at, :] = tile
                top[at, :] = tile if first else jnp.maximum(top[at, :], tile)

    score(me, True)
    for which in range(2):
        own_copy(which, 0, sibling).wait_recv()
    score(sibling, False)

    def direct_turn(k, carry):
        source = shifted(k + 1, -1) * 2 + core
        for which in range(2):
            own_copy(which, k + 1, source).wait_recv()
            pass_copy(which, k + 1, source).start()
        score(source, False)
        return carry

    repeat(chips - 1, direct_turn)

    def passed_turn(k, carry):
        source = shifted(k + 1, -1) * 2 + 1 - core
        for which in range(2):
            pass_copy(which, k + 1, source).wait_recv()
        score(source, False)
        return carry

    repeat(chips - 1, passed_turn)

    wide = jnp.zeros((rows, LANES), jnp.float32)
    for head in range(heads):
        at = pl.ds(head * rows, rows)
        t_high = jnp.max(t_top[at, :], axis=1, keepdims=True)
        s_high = jnp.max(s_top[at, :], axis=1, keepdims=True)
        blank = jnp.zeros((rows, LANES), jnp.float32)

        def sum_turn(block, carry):
            t_sum, s_sum, gap_sum = carry
            t_tile, s_tile = t_scores[block, at, :], s_scores[block, at, :]
            t_exp = jnp.exp2(t_tile - t_high)
            return (
                t_sum + t_exp,
                s_sum + jnp.exp2(s_tile - s_high),
                gap_sum + t_exp * (t_tile - s_tile),
            )

        t_sum, s_sum, gap_sum = [
            jnp.sum(part, axis=1, keepdims=True)
            for part in repeat(n, sum_turn, (blank, blank, blank))
        ]
        t_line = t_high + jnp.log2(t_sum)
        s_line = s_high + jnp.log2(s_sum)
        div_line = gap_sum / t_sum - t_line + s_line
        t_log[at, :] = jnp.broadcast_to(t_line, (rows, LANES))
        s_log[at, :] = jnp.broadcast_to(s_line, (rows, LANES))
        wide = jnp.where(lane == head, t_line, wide)
        wide = jnp.where(lane == heads + head, s_line, wide)
        wide = jnp.where(lane == 2 * heads + head, div_line, wide)
    stats[me] = wide.T[: stats.shape[1]]

    def stat_copy(d, target):
        return pltpu.make_async_remote_copy(
            src_ref=stats.at[me],
            dst_ref=stats.at[me],
            send_sem=stat_send.at[d],
            recv_sem=stat_recv.at[d],
            device_id=spot(target),
            device_id_type=MESH,
        )

    def send_stats(d, carry):
        stat_copy(d + 1, (me + d + 1) % n).start()
        return carry

    repeat(n - 1, send_stats)

    def row_turn(block, carry):
        for head in range(heads):
            at = pl.ds(head * rows, rows)
            row_part[block, at, :] = jnp.exp2(s_scores[block, at, :] - s_log[at, :]) - jnp.exp2(
                t_scores[block, at, :] - t_log[at, :]
            )
        return carry

    repeat(n, row_turn)

    def gradient(block, first):
        for pair in range(pairs):
            parts = []
            for inner in range(group):
                head = pair * group + inner
                at = pl.ds(head * rows, rows)
                t_line = stats[block, pl.ds(head, 1), :]
                s_line = stats[block, pl.ds(heads + head, 1), :]
                column_part = jnp.exp2(s_scores[block, at, :] - s_line) - jnp.exp2(
                    t_scores[block, at, :] - t_line
                )
                parts.append((row_part[block, at, :] + column_part).astype(jnp.bfloat16))
            at = pl.ds(pair * group * rows, group * rows)
            piece = jnp.dot(
                jnp.concatenate(parts, axis=0),
                student[block, :, pl.ds(pair * LANES, LANES)],
                preferred_element_type=jnp.float32,
            )
            total[at, :] = piece if first else total[at, :] + piece

    gradient(me, True)

    def gradient_turn(d, carry):
        source = (me - d - 1 + n) % n
        stat_copy(d + 1, source).wait_recv()
        gradient(source, False)
        return carry

    repeat(n - 1, gradient_turn)

    for pair in range(pairs):
        chosen = total[pl.ds(pair * group * rows, rows), :]
        for inner in range(1, group):
            chosen = jnp.where(
                lane // HEAD_DIM == inner,
                total[pl.ds((pair * group + inner) * rows, rows), :],
                chosen,
            )
        grad_ref[:, pl.ds(pair * LANES, LANES)] = (
            chosen * (distill_weight * HEAD_DIM ** (-0.5))
        ).astype(jnp.bfloat16)

    def div_turn(block, carry):
        return carry + stats[block]

    div_sum = repeat(n, div_turn, jnp.zeros(stats.shape[1:], jnp.float32))
    div_sum = jnp.sum(div_sum, axis=1, keepdims=True) * (math.log(2.0) / (rows * n))
    row_at = lax.broadcasted_iota(jnp.int32, stats.shape[1:], 0)
    lane_at = lax.broadcasted_iota(jnp.int32, stats.shape[1:], 1)
    div_row = jnp.sum(
        jnp.where(row_at == 2 * heads + lane_at, div_sum, 0.0), axis=0, keepdims=True
    )
    div_ref[...] = div_row[:, :heads]

    for which in range(2):
        own_copy(which, 0, sibling).wait_send()

    def drain(k, carry):
        for which in range(2):
            own_copy(which, k + 1, sibling).wait_send()
            pass_copy(which, k + 1, me).wait_send()
        return carry

    repeat(chips - 1, drain)

    def drain_stats(d, carry):
        stat_copy(d + 1, sibling).wait_send()
        return carry

    repeat(n - 1, drain_stats)


def per_device(n, teacher_q, student_q, owner_table):
    rows, width = teacher_q.shape
    heads = width // HEAD_DIM
    chips = n // 2
    stat_rows = -(-3 * heads // 8) * 8
    hbm = pl.BlockSpec(memory_space=pl.ANY)
    grad, divergence = pl.pallas_call(
        functools.partial(kernel, n),
        out_shape=(
            jax.ShapeDtypeStruct((rows, width), jnp.bfloat16),
            jax.ShapeDtypeStruct((1, heads), jnp.float32),
        ),
        in_specs=[hbm, hbm, pl.BlockSpec(memory_space=pltpu.SMEM)],
        out_specs=(
            pl.BlockSpec(memory_space=pltpu.VMEM),
            pl.BlockSpec(memory_space=pltpu.VMEM),
        ),
        scratch_shapes=[
            pltpu.VMEM((n, rows, width), jnp.bfloat16),
            pltpu.VMEM((n, rows, width), jnp.bfloat16),
            pltpu.VMEM((heads * rows, LANES), jnp.bfloat16),
            pltpu.VMEM((heads * rows, LANES), jnp.bfloat16),
            pltpu.VMEM((n, heads * rows, rows), jnp.float32),
            pltpu.VMEM((n, heads * rows, rows), jnp.float32),
            pltpu.VMEM((heads * rows, rows), jnp.float32),
            pltpu.VMEM((heads * rows, rows), jnp.float32),
            pltpu.VMEM((heads * rows, LANES), jnp.float32),
            pltpu.VMEM((heads * rows, LANES), jnp.float32),
            pltpu.VMEM((n, heads * rows, rows), jnp.float32),
            pltpu.VMEM((n, stat_rows, rows), jnp.float32),
            pltpu.VMEM((heads * rows, LANES), jnp.float32),
            pltpu.SemaphoreType.DMA((2,)),
            pltpu.SemaphoreType.DMA((2, chips)),
            pltpu.SemaphoreType.DMA((2, chips)),
            pltpu.SemaphoreType.DMA((2, chips)),
            pltpu.SemaphoreType.DMA((2, chips)),
            pltpu.SemaphoreType.DMA((n,)),
            pltpu.SemaphoreType.DMA((n,)),
        ],
        compiler_params=pltpu.CompilerParams(
            collective_id=0, has_side_effects=True, vmem_limit_bytes=60 * 1024 * 1024
        ),
        name="distill",
    )(teacher_q, student_q, owner_table)
    return (grad, divergence.reshape(heads))


def solution(mesh):
    placed = (P("tok", "head"), P("tok", "head"), P())
    return jax.shard_map(
        functools.partial(per_device, mesh.shape["tok"]),
        mesh=mesh,
        in_specs=placed,
        out_specs=(P("tok", "head"), P("head")),
        check_vma=False,
    )
```

```python
import functools
import math

import jax
import jax.numpy as jnp
from jax import lax
from jax.experimental import pallas as pl
from jax.experimental.pallas import tpu as pltpu
from jax.sharding import PartitionSpec as P

HEAD_DIM = 64
LANES = 128
floor_value = -1e30
distill_weight = 32.0
score_factor = HEAD_DIM ** (-0.5) * math.log2(math.e)
MESH = pl.DeviceIdType.MESH


def repeat(count, body, init=None):
    if count <= 8:
        for step in range(count):
            init = body(step, init)
        return init
    return lax.fori_loop(0, count, body, init)


def kernel(
    n, teacher_hbm, student_hbm, table, grad_ref, div_ref,
    teacher, student, outbox, inbox, own, scores, top, logs, row_part, stats, total,
    out_grad, in_grad, out_div, in_div,
    local_sem, send_sem, recv_sem, stat_send, stat_recv, back_send, back_recv,
):
    rows, width = teacher_hbm.shape
    pairs = width // LANES
    heads = width // HEAD_DIM
    group = LANES // HEAD_DIM
    parts = n // heads
    chips = n // 2
    side = math.isqrt(chips)
    side = side if side * side == chips else 1
    span = chips // side
    half = rows // 2
    own_rows = heads * rows
    me = lax.axis_index("tok")
    head_at = lax.axis_index("head")
    chip, core = me // 2, me % 2
    head, part = me // parts, me % parts

    def spot(tok):
        return (head_at, tok)

    def shifted(k, sign):
        high = (chip // span + sign * (k // span) + side) % side
        low = (chip % span + sign * (k % span) + span) % span
        return high * span + low

    def remote(src, dst, send, recv, target):
        return pltpu.make_async_remote_copy(
            src_ref=src, dst_ref=dst, send_sem=send, recv_sem=recv,
            device_id=spot(target), device_id_type=MESH,
        )

    barrier = pltpu.get_barrier_semaphore()
    loads = [
        pltpu.make_async_copy(teacher_hbm, teacher, local_sem.at[0]),
        pltpu.make_async_copy(student_hbm, student, local_sem.at[1]),
    ]
    for load in loads:
        load.start()

    def greet(d, carry):
        pl.semaphore_signal(barrier, inc=1, device_id=spot((me + d + 1) % n), device_id_type=MESH)
        return carry

    repeat(n - 1, greet)
    for load in loads:
        load.wait()
    lane = lax.broadcasted_iota(jnp.int32, (rows, LANES), 1)
    lower = lane < HEAD_DIM
    for pair in range(pairs):
        columns = pl.ds(pair * LANES, LANES)
        t_pair = teacher[:, columns].astype(jnp.float32)
        s_pair = student[:, columns].astype(jnp.float32)
        outbox[pair * group] = jnp.where(lower, t_pair, pltpu.roll(s_pair, HEAD_DIM, 1)).astype(
            jnp.bfloat16
        )
        outbox[pair * group + 1] = jnp.where(
            lower, pltpu.roll(t_pair, HEAD_DIM, 1), s_pair
        ).astype(jnp.bfloat16)
    inbox[pl.ds(me * rows, rows), :] = outbox[head]
    pl.semaphore_wait(barrier, n - 1)

    def query_copy(k, other, target):
        return remote(
            outbox.at[target // parts],
            inbox.at[pl.ds(me * rows, rows), :],
            send_sem.at[k, other],
            recv_sem.at[k, other],
            target,
        )

    def away(k, other, sign):
        return shifted(k, sign) * 2 + (1 - core if other else core)

    def send_queries(step, carry):
        k = chips - 1 - step
        for other in range(2):
            query_copy(k, other, away(k, other, 1)).start()
        return carry

    repeat(chips - 1, send_queries)
    query_copy(0, 1, away(0, 1, 1)).start()

    query_copy(0, 1, away(0, 1, -1)).wait_recv()

    def take_queries(step, carry):
        for other in range(2):
            query_copy(step + 1, other, away(step + 1, other, -1)).wait_recv()
        return carry

    repeat(chips - 1, take_queries)

    none = jnp.zeros((), jnp.bfloat16)
    for place in range(heads):
        block = inbox[pl.ds((part * heads + place) * rows, rows), :]
        own[pl.ds(place * rows, rows), :] = jnp.where(lower, block, none)
        own[pl.ds(own_rows + place * rows, rows), :] = jnp.where(lower, none, block)

    top[...] = jnp.full(top.shape, 2 * floor_value, jnp.float32)

    def score_turn(step, carry):
        right = inbox[pl.ds(step * 2 * rows, 2 * rows), :]
        raw = lax.dot_general(
            own[...], right, (((1,), (1,)), ((), ())), preferred_element_type=jnp.float32
        )
        for place in range(heads):
            for near in range(2):
                block = step * 2 + near
                bias = jnp.where(table[part * heads + place, block] >= 0, 0.0, floor_value)
                for which in range(2):
                    begin = which * own_rows + place * rows
                    at = pl.ds(begin, rows)
                    tile = (
                        raw[begin : begin + rows, near * rows : (near + 1) * rows] * score_factor
                        + bias.astype(jnp.float32)
                    )
                    scores[block, at, :] = tile
                    top[at, :] = jnp.maximum(top[at, :], tile)
        return carry

    repeat(n // 2, score_turn)

    wide = jnp.zeros((rows, LANES), jnp.float32)
    for place in range(heads):
        t_at, s_at = pl.ds(place * rows, rows), pl.ds(own_rows + place * rows, rows)
        t_high = jnp.max(top[t_at, :], axis=1, keepdims=True)
        s_high = jnp.max(top[s_at, :], axis=1, keepdims=True)
        blank = jnp.zeros((rows, LANES), jnp.float32)

        def sum_turn(block, carry):
            t_sum, s_sum, gap_sum = carry
            t_tile, s_tile = scores[block, t_at, :], scores[block, s_at, :]
            t_exp = jnp.exp2(t_tile - t_high)
            return (
                t_sum + t_exp,
                s_sum + jnp.exp2(s_tile - s_high),
                gap_sum + t_exp * (t_tile - s_tile),
            )

        t_sum, s_sum, gap_sum = [
            jnp.sum(piece, axis=1, keepdims=True)
            for piece in repeat(n, sum_turn, (blank, blank, blank))
        ]
        t_line = t_high + jnp.log2(t_sum)
        s_line = s_high + jnp.log2(s_sum)
        div_line = gap_sum / t_sum - t_line + s_line
        logs[t_at, :] = jnp.broadcast_to(t_line, (rows, LANES))
        logs[s_at, :] = jnp.broadcast_to(s_line, (rows, LANES))
        wide = jnp.where(lane == place, t_line, wide)
        wide = jnp.where(lane == heads + place, s_line, wide)
        wide = jnp.where(lane == 2 * heads + place, div_line, wide)
    stats[part] = wide.T[: stats.shape[1]]

    def stat_copy(step, target):
        return remote(
            stats.at[part], stats.at[part], stat_send.at[step], stat_recv.at[step], target
        )

    def send_stats(step, carry):
        stat_copy(step, head * parts + (part + step + 1) % parts).start()
        return carry

    repeat(parts - 1, send_stats)

    def row_turn(block, carry):
        for place in range(heads):
            t_at, s_at = pl.ds(place * rows, rows), pl.ds(own_rows + place * rows, rows)
            row_part[block, t_at, :] = jnp.exp2(scores[block, s_at, :] - logs[s_at, :]) - jnp.exp2(
                scores[block, t_at, :] - logs[t_at, :]
            )
        return carry

    repeat(n, row_turn)

    def take_stats(step, carry):
        stat_copy(step, head * parts + (part - step - 1 + parts) % parts).wait_recv()
        return carry

    repeat(parts - 1, take_stats)

    def div_turn(step, carry):
        return carry + stats[step, pl.ds(2 * heads, heads), :]

    div_sum = repeat(parts, div_turn, jnp.zeros((heads, rows), jnp.float32))
    div_sum = jnp.sum(jnp.sum(div_sum, axis=0, keepdims=True), axis=1, keepdims=True)
    out_div[...] = jnp.broadcast_to(div_sum * (math.log(2.0) / (rows * n)), out_div.shape)

    def div_copy(place, slot, target):
        return remote(out_div, in_div.at[head], back_send.at[1, place], back_recv.at[1, slot], target)

    def grad_copy(place, slot, target):
        return remote(
            out_grad.at[place], in_grad.at[head], back_send.at[0, place], back_recv.at[0, slot], target
        )

    for place in range(heads):
        target = part * heads + place

        @pl.when(target != me)
        def send_div():
            div_copy(place, head, target).start()

        @pl.when(target == me)
        def keep_div():
            in_div[head] = out_div[...]

    def gradient_turn(step, carry):
        lines = []
        for place in range(heads):
            t_at, s_at = pl.ds(place * rows, rows), pl.ds(own_rows + place * rows, rows)
            pieces = []
            for near in range(2):
                block = step * 2 + near
                line = stats.at[block // heads]
                t_line = line[pl.ds(block % heads, 1), :]
                s_line = line[pl.ds(heads + block % heads, 1), :]
                column_part = jnp.exp2(scores[block, s_at, :] - s_line) - jnp.exp2(
                    scores[block, t_at, :] - t_line
                )
                pieces.append((row_part[block, t_at, :] + column_part).astype(jnp.bfloat16))
            lines.append(jnp.concatenate(pieces, axis=1))
        piece = jnp.dot(
            jnp.concatenate(lines, axis=0),
            inbox[pl.ds(step * 2 * rows, 2 * rows), :],
            preferred_element_type=jnp.float32,
        )
        total[...] = piece if isinstance(step, int) and step == 0 else total[...] + piece
        return carry

    if n // 2 > 8:
        total[...] = jnp.zeros(total.shape, jnp.float32)
    repeat(n // 2, gradient_turn)

    half_lower = lax.broadcasted_iota(jnp.int32, (half, LANES), 1) < HEAD_DIM
    for place in range(heads):
        target = part * heads + place
        upper_rows = total[pl.ds(place * rows, half), :]
        lower_rows = total[pl.ds(place * rows + half, half), :]
        out_grad[place] = (
            jnp.where(half_lower, pltpu.roll(upper_rows, HEAD_DIM, 1), lower_rows)
            * (distill_weight * HEAD_DIM ** (-0.5))
        ).astype(jnp.bfloat16)

        @pl.when(target != me)
        def send_grad():
            grad_copy(place, head, target).start()

        @pl.when(target == me)
        def keep_grad():
            in_grad[head] = out_grad[place]

    for slot in range(heads):
        source = slot * parts + me // heads

        @pl.when(source != me)
        def take_back():
            div_copy(0, slot, source).wait_recv()
            grad_copy(0, slot, source).wait_recv()

    for pair in range(pairs):
        first = in_grad[pair * group].astype(jnp.float32)
        second = in_grad[pair * group + 1].astype(jnp.float32)
        columns = pl.ds(pair * LANES, LANES)
        grad_ref[pl.ds(0, half), columns] = jnp.where(
            half_lower, first, pltpu.roll(second, HEAD_DIM, 1)
        ).astype(jnp.bfloat16)
        grad_ref[pl.ds(half, half), columns] = jnp.where(
            half_lower, pltpu.roll(first, HEAD_DIM, 1), second
        ).astype(jnp.bfloat16)
    div_lane = lax.broadcasted_iota(jnp.int32, (1, LANES), 1)
    div_row = jnp.zeros((1, LANES), jnp.float32)
    for slot in range(heads):
        div_row = jnp.where(div_lane == slot, in_div[slot, pl.ds(0, 1), :], div_row)
    div_ref[...] = div_row[:, :heads]

    query_copy(0, 1, away(0, 1, 1)).wait_send()

    def drain(step, carry):
        for other in range(2):
            query_copy(step + 1, other, away(step + 1, other, 1)).wait_send()
        return carry

    repeat(chips - 1, drain)

    def drain_stats(step, carry):
        stat_copy(step, head * parts + (part + step + 1) % parts).wait_send()
        return carry

    repeat(parts - 1, drain_stats)
    for place in range(heads):
        target = part * heads + place

        @pl.when(target != me)
        def drain_back():
            div_copy(place, head, target).wait_send()
            grad_copy(place, head, target).wait_send()


def per_device(n, teacher_q, student_q, owner_table):
    rows, width = teacher_q.shape
    heads = width // HEAD_DIM
    chips = n // 2
    parts = n // heads
    stat_rows = -(-3 * heads // 8) * 8
    hbm = pl.BlockSpec(memory_space=pl.ANY)
    grad, divergence = pl.pallas_call(
        functools.partial(kernel, n),
        out_shape=(
            jax.ShapeDtypeStruct((rows, width), jnp.bfloat16),
            jax.ShapeDtypeStruct((1, heads), jnp.float32),
        ),
        in_specs=[hbm, hbm, pl.BlockSpec(memory_space=pltpu.SMEM)],
        out_specs=(
            pl.BlockSpec(memory_space=pltpu.VMEM),
            pl.BlockSpec(memory_space=pltpu.VMEM),
        ),
        scratch_shapes=[
            pltpu.VMEM((rows, width), jnp.bfloat16),
            pltpu.VMEM((rows, width), jnp.bfloat16),
            pltpu.VMEM((heads, rows, LANES), jnp.bfloat16),
            pltpu.VMEM((n * rows, LANES), jnp.bfloat16),
            pltpu.VMEM((2 * heads * rows, LANES), jnp.bfloat16),
            pltpu.VMEM((n, 2 * heads * rows, rows), jnp.float32),
            pltpu.VMEM((2 * heads * rows, rows), jnp.float32),
            pltpu.VMEM((2 * heads * rows, LANES), jnp.float32),
            pltpu.VMEM((n, heads * rows, rows), jnp.float32),
            pltpu.VMEM((parts, stat_rows, rows), jnp.float32),
            pltpu.VMEM((heads * rows, LANES), jnp.float32),
            pltpu.VMEM((heads, rows // 2, LANES), jnp.bfloat16),
            pltpu.VMEM((heads, rows // 2, LANES), jnp.bfloat16),
            pltpu.VMEM((8, LANES), jnp.float32),
            pltpu.VMEM((heads, 8, LANES), jnp.float32),
            pltpu.SemaphoreType.DMA((2,)),
            pltpu.SemaphoreType.DMA((chips, 2)),
            pltpu.SemaphoreType.DMA((chips, 2)),
            pltpu.SemaphoreType.DMA((parts,)),
            pltpu.SemaphoreType.DMA((parts,)),
            pltpu.SemaphoreType.DMA((2, heads)),
            pltpu.SemaphoreType.DMA((2, heads)),
        ],
        compiler_params=pltpu.CompilerParams(
            collective_id=0, has_side_effects=True, vmem_limit_bytes=60 * 1024 * 1024
        ),
        name="distill",
    )(teacher_q, student_q, owner_table)
    return (grad, divergence.reshape(heads))


def solution(mesh):
    placed = (P("tok", "head"), P("tok", "head"), P())
    return jax.shard_map(
        functools.partial(per_device, mesh.shape["tok"]),
        mesh=mesh,
        in_specs=placed,
        out_specs=(P("tok", "head"), P("head")),
        check_vma=False,
    )
```

```python
import functools
import math

import jax
import jax.numpy as jnp
from jax import lax
from jax.experimental import pallas as pl
from jax.experimental.pallas import tpu as pltpu
from jax.sharding import PartitionSpec as P

HEAD_DIM = 64
LANES = 128
floor_value = -1e30
distill_weight = 32.0
score_factor = HEAD_DIM ** (-0.5) * math.log2(math.e)
MESH = pl.DeviceIdType.MESH


def repeat(count, body, init=None):
    if count <= 8:
        for step in range(count):
            init = body(step, init)
        return init
    return lax.fori_loop(0, count, body, init)


def kernel(
    n, teacher_hbm, student_hbm, table, in_grad, in_div,
    teacher, student, outbox, inbox, own, scores, top, logs, row_part, stats,
    out_grad, out_div, local_sem, send_sem, recv_sem, stat_send, stat_recv, back_send, back_recv,
):
    rows, width = teacher_hbm.shape
    pairs = width // LANES
    heads = width // HEAD_DIM
    group = LANES // HEAD_DIM
    parts = n // heads
    chips = n // 2
    side = math.isqrt(chips)
    side = side if side * side == chips else 1
    span = chips // side
    half = rows // 2
    own_rows = heads * rows
    me = lax.axis_index("tok")
    head_at = lax.axis_index("head")
    chip, core = me // 2, me % 2
    head, part = me // parts, me % parts

    def spot(tok):
        return (head_at, tok)

    def shifted(k, sign):
        high = (chip // span + sign * (k // span) + side) % side
        low = (chip % span + sign * (k % span) + span) % span
        return high * span + low

    def remote(src, dst, send, recv, target):
        return pltpu.make_async_remote_copy(
            src_ref=src, dst_ref=dst, send_sem=send, recv_sem=recv,
            device_id=spot(target), device_id_type=MESH,
        )

    barrier = pltpu.get_barrier_semaphore()
    loads = [
        pltpu.make_async_copy(teacher_hbm, teacher, local_sem.at[0]),
        pltpu.make_async_copy(student_hbm, student, local_sem.at[1]),
    ]
    for load in loads:
        load.start()

    def greet(d, carry):
        pl.semaphore_signal(barrier, inc=1, device_id=spot((me + d + 1) % n), device_id_type=MESH)
        return carry

    repeat(n - 1, greet)
    for load in loads:
        load.wait()
    lane = lax.broadcasted_iota(jnp.int32, (rows, LANES), 1)
    lower = lane < HEAD_DIM
    for pair in range(pairs):
        columns = pl.ds(pair * LANES, LANES)
        t_pair = teacher[:, columns].astype(jnp.float32)
        s_pair = student[:, columns].astype(jnp.float32)
        outbox[pair * group] = jnp.where(lower, t_pair, pltpu.roll(s_pair, HEAD_DIM, 1)).astype(
            jnp.bfloat16
        )
        outbox[pair * group + 1] = jnp.where(
            lower, pltpu.roll(t_pair, HEAD_DIM, 1), s_pair
        ).astype(jnp.bfloat16)
    inbox[pl.ds(me * rows, rows), :] = outbox[head]
    pl.semaphore_wait(barrier, n - 1)

    def query_copy(k, other, target):
        return remote(
            outbox.at[target // parts],
            inbox.at[pl.ds(me * rows, rows), :],
            send_sem.at[k, other],
            recv_sem.at[k, other],
            target,
        )

    def away(k, other, sign):
        return shifted(k, sign) * 2 + (1 - core if other else core)

    def send_queries(step, carry):
        k = chips - 1 - step
        for other in range(2):
            query_copy(k, other, away(k, other, 1)).start()
        return carry

    repeat(chips - 1, send_queries)
    query_copy(0, 1, away(0, 1, 1)).start()

    query_copy(0, 1, away(0, 1, -1)).wait_recv()

    def take_queries(step, carry):
        for other in range(2):
            query_copy(step + 1, other, away(step + 1, other, -1)).wait_recv()
        return carry

    repeat(chips - 1, take_queries)

    none = jnp.zeros((), jnp.bfloat16)
    for place in range(heads):
        block = inbox[pl.ds((part * heads + place) * rows, rows), :]
        own[pl.ds(place * rows, rows), :] = jnp.where(lower, block, none)
        own[pl.ds(own_rows + place * rows, rows), :] = jnp.where(lower, none, block)

    top[...] = jnp.full(top.shape, 2 * floor_value, jnp.float32)

    def score_turn(step, carry):
        right = inbox[pl.ds(step * 2 * rows, 2 * rows), :]
        raw = lax.dot_general(
            own[...], right, (((1,), (1,)), ((), ())), preferred_element_type=jnp.float32
        )
        for place in range(heads):
            for near in range(2):
                block = step * 2 + near
                bias = jnp.where(table[part * heads + place, block] >= 0, 0.0, floor_value)
                for which in range(2):
                    begin = which * own_rows + place * rows
                    at = pl.ds(begin, rows)
                    tile = (
                        raw[begin : begin + rows, near * rows : (near + 1) * rows] * score_factor
                        + bias.astype(jnp.float32)
                    )
                    scores[block, at, :] = tile
                    top[at, :] = jnp.maximum(top[at, :], tile)
        return carry

    repeat(n // 2, score_turn)

    wide = jnp.zeros((rows, LANES), jnp.float32)
    for place in range(heads):
        t_at, s_at = pl.ds(place * rows, rows), pl.ds(own_rows + place * rows, rows)
        t_high = jnp.max(top[t_at, :], axis=1, keepdims=True)
        s_high = jnp.max(top[s_at, :], axis=1, keepdims=True)
        blank = jnp.zeros((rows, LANES), jnp.float32)

        def sum_turn(block, carry):
            t_sum, s_sum, gap_sum = carry
            t_tile, s_tile = scores[block, t_at, :], scores[block, s_at, :]
            t_exp = jnp.exp2(t_tile - t_high)
            return (
                t_sum + t_exp,
                s_sum + jnp.exp2(s_tile - s_high),
                gap_sum + t_exp * (t_tile - s_tile),
            )

        t_sum, s_sum, gap_sum = [
            jnp.sum(piece, axis=1, keepdims=True)
            for piece in repeat(n, sum_turn, (blank, blank, blank))
        ]
        t_line = t_high + jnp.log2(t_sum)
        s_line = s_high + jnp.log2(s_sum)
        div_line = gap_sum / t_sum - t_line + s_line
        logs[t_at, :] = jnp.broadcast_to(t_line, (rows, LANES))
        logs[s_at, :] = jnp.broadcast_to(s_line, (rows, LANES))
        wide = jnp.where(lane == place, t_line, wide)
        wide = jnp.where(lane == heads + place, s_line, wide)
        wide = jnp.where(lane == 2 * heads + place, div_line, wide)
    stats[part] = wide.T[: stats.shape[1]]

    def stat_copy(step, target):
        return remote(
            stats.at[part], stats.at[part], stat_send.at[step], stat_recv.at[step], target
        )

    def send_stats(step, carry):
        stat_copy(step, head * parts + (part + step + 1) % parts).start()
        return carry

    repeat(parts - 1, send_stats)

    def row_turn(block, carry):
        for place in range(heads):
            t_at, s_at = pl.ds(place * rows, rows), pl.ds(own_rows + place * rows, rows)
            row_part[block, t_at, :] = jnp.exp2(scores[block, s_at, :] - logs[s_at, :]) - jnp.exp2(
                scores[block, t_at, :] - logs[t_at, :]
            )
        return carry

    repeat(n, row_turn)

    def take_stats(step, carry):
        stat_copy(step, head * parts + (part - step - 1 + parts) % parts).wait_recv()
        return carry

    repeat(parts - 1, take_stats)

    def div_turn(step, carry):
        return carry + stats[step, pl.ds(2 * heads, heads), :]

    div_sum = repeat(parts, div_turn, jnp.zeros((heads, rows), jnp.float32))
    div_sum = jnp.sum(jnp.sum(div_sum, axis=0, keepdims=True), axis=1, keepdims=True)
    out_div[...] = jnp.broadcast_to(div_sum * (math.log(2.0) / (rows * n)), out_div.shape)

    def div_copy(place, slot, target):
        return remote(out_div, in_div.at[head], back_send.at[1, place], back_recv.at[1, slot], target)

    def grad_copy(place, slot, target):
        return remote(
            out_grad.at[place], in_grad.at[head], back_send.at[0, place], back_recv.at[0, slot], target
        )

    for place in range(heads):
        target = part * heads + place

        @pl.when(target != me)
        def send_div():
            div_copy(place, head, target).start()

        @pl.when(target == me)
        def keep_div():
            keep = pltpu.make_async_copy(out_div, in_div.at[head], local_sem.at[0])
            keep.start()
            keep.wait()

    half_lower = lax.broadcasted_iota(jnp.int32, (half, LANES), 1) < HEAD_DIM
    run = heads // 2
    for turn in range(2):
        place_base = (chip + 1 + turn) % 2 * run

        def gradient_turn(step, carry):
            lines = []
            for inner in range(run):
                place = place_base + inner
                t_at = pl.ds(pl.multiple_of(place * rows, rows), rows)
                s_at = pl.ds(pl.multiple_of(own_rows + place * rows, rows), rows)
                pieces = []
                for near in range(2):
                    block = step * 2 + near
                    line = stats.at[block // heads]
                    t_line = line[pl.ds(block % heads, 1), :]
                    s_line = line[pl.ds(heads + block % heads, 1), :]
                    column_part = jnp.exp2(scores[block, s_at, :] - s_line) - jnp.exp2(
                        scores[block, t_at, :] - t_line
                    )
                    pieces.append((row_part[block, t_at, :] + column_part).astype(jnp.bfloat16))
                lines.append(jnp.concatenate(pieces, axis=1))
            return carry + jnp.dot(
                jnp.concatenate(lines, axis=0),
                inbox[pl.ds(step * 2 * rows, 2 * rows), :],
                preferred_element_type=jnp.float32,
            )

        total = repeat(n // 2, gradient_turn, jnp.zeros((run * rows, LANES), jnp.float32))
        for inner in range(run):
            place = place_base + inner
            target = part * heads + place
            upper_rows = total[inner * rows : inner * rows + half]
            lower_rows = total[inner * rows + half : (inner + 1) * rows]
            out_grad[place] = (
                jnp.where(half_lower, pltpu.roll(upper_rows, HEAD_DIM, 1), lower_rows)
                * (distill_weight * HEAD_DIM ** (-0.5))
            ).astype(jnp.bfloat16)

            @pl.when(target != me)
            def send_grad():
                grad_copy(place, head, target).start()

    @pl.when(part == me // heads)
    def keep_grad():
        keep = pltpu.make_async_copy(out_grad.at[me % heads], in_grad.at[head], local_sem.at[1])
        keep.start()
        keep.wait()

    for slot in range(heads):
        source = slot * parts + me // heads

        @pl.when(source != me)
        def take_back():
            div_copy(0, slot, source).wait_recv()
            grad_copy(0, slot, source).wait_recv()

    query_copy(0, 1, away(0, 1, 1)).wait_send()

    def drain(step, carry):
        for other in range(2):
            query_copy(step + 1, other, away(step + 1, other, 1)).wait_send()
        return carry

    repeat(chips - 1, drain)

    def drain_stats(step, carry):
        stat_copy(step, head * parts + (part + step + 1) % parts).wait_send()
        return carry

    repeat(parts - 1, drain_stats)
    for place in range(heads):
        target = part * heads + place

        @pl.when(target != me)
        def drain_back():
            div_copy(place, head, target).wait_send()
            grad_copy(place, head, target).wait_send()


def unpack(in_grad, in_div, grad_ref, div_ref):
    heads, half = in_grad.shape[:2]
    group = LANES // HEAD_DIM
    half_lower = lax.broadcasted_iota(jnp.int32, (half, LANES), 1) < HEAD_DIM
    for pair in range(heads // group):
        first = in_grad[pair * group].astype(jnp.float32)
        second = in_grad[pair * group + 1].astype(jnp.float32)
        columns = pl.ds(pair * LANES, LANES)
        grad_ref[pl.ds(0, half), columns] = jnp.where(
            half_lower, first, pltpu.roll(second, HEAD_DIM, 1)
        ).astype(jnp.bfloat16)
        grad_ref[pl.ds(half, half), columns] = jnp.where(
            half_lower, pltpu.roll(first, HEAD_DIM, 1), second
        ).astype(jnp.bfloat16)
    div_lane = lax.broadcasted_iota(jnp.int32, (1, LANES), 1)
    div_row = jnp.zeros((1, LANES), jnp.float32)
    for slot in range(heads):
        div_row = jnp.where(div_lane == slot, in_div[slot, pl.ds(0, 1), :], div_row)
    div_ref[...] = div_row[:, :heads]


def per_device(n, teacher_q, student_q, owner_table):
    rows, width = teacher_q.shape
    heads = width // HEAD_DIM
    chips = n // 2
    parts = n // heads
    stat_rows = -(-3 * heads // 8) * 8
    hbm = pl.BlockSpec(memory_space=pl.ANY)
    packed = pl.pallas_call(
        functools.partial(kernel, n),
        out_shape=(
            jax.ShapeDtypeStruct((heads, rows // 2, LANES), jnp.bfloat16),
            jax.ShapeDtypeStruct((heads, 8, LANES), jnp.float32),
        ),
        in_specs=[hbm, hbm, pl.BlockSpec(memory_space=pltpu.SMEM)],
        out_specs=(hbm, hbm),
        scratch_shapes=[
            pltpu.VMEM((rows, width), jnp.bfloat16),
            pltpu.VMEM((rows, width), jnp.bfloat16),
            pltpu.VMEM((heads, rows, LANES), jnp.bfloat16),
            pltpu.VMEM((n * rows, LANES), jnp.bfloat16),
            pltpu.VMEM((2 * heads * rows, LANES), jnp.bfloat16),
            pltpu.VMEM((n, 2 * heads * rows, rows), jnp.float32),
            pltpu.VMEM((2 * heads * rows, rows), jnp.float32),
            pltpu.VMEM((2 * heads * rows, LANES), jnp.float32),
            pltpu.VMEM((n, heads * rows, rows), jnp.float32),
            pltpu.VMEM((parts, stat_rows, rows), jnp.float32),
            pltpu.VMEM((heads, rows // 2, LANES), jnp.bfloat16),
            pltpu.VMEM((8, LANES), jnp.float32),
            pltpu.SemaphoreType.DMA((2,)),
            pltpu.SemaphoreType.DMA((chips, 2)),
            pltpu.SemaphoreType.DMA((chips, 2)),
            pltpu.SemaphoreType.DMA((parts,)),
            pltpu.SemaphoreType.DMA((parts,)),
            pltpu.SemaphoreType.DMA((2, heads)),
            pltpu.SemaphoreType.DMA((2, heads)),
        ],
        compiler_params=pltpu.CompilerParams(
            collective_id=0, has_side_effects=True, vmem_limit_bytes=60 * 1024 * 1024
        ),
        name="distill",
    )(teacher_q, student_q, owner_table)
    grad, divergence = pl.pallas_call(
        unpack,
        out_shape=(
            jax.ShapeDtypeStruct((rows, width), jnp.bfloat16),
            jax.ShapeDtypeStruct((1, heads), jnp.float32),
        ),
        in_specs=[pl.BlockSpec(memory_space=pltpu.VMEM)] * 2,
        out_specs=(pl.BlockSpec(memory_space=pltpu.VMEM),) * 2,
        name="unpack",
    )(*packed)
    return (grad, divergence.reshape(heads))


def solution(mesh):
    placed = (P("tok", "head"), P("tok", "head"), P())
    return jax.shard_map(
        functools.partial(per_device, mesh.shape["tok"]),
        mesh=mesh,
        in_specs=placed,
        out_specs=(P("tok", "head"), P("head")),
        check_vma=False,
    )
```
